32 devices in a mesh: groups: 2 (over x), rows: 16 (over z, y, core).
Axes of the slice: x: 2, y: 2, z: 4, core: 2. Of those that a mesh axis runs over, the one named last changes fastest.
Arguments:
- skip_input: bfloat16 [256, 64, 640], P(('groups', 'rows')), parts along dimension 0, may hold values from -4 to 4
- conv_hidden: bfloat16 [256, 64, 640], P(('groups', 'rows')), parts along dimension 0, may hold values from -108 to 108, as said below
- noise_target: bfloat16 [256, 64, 640], P(('groups', 'rows')), parts along dimension 0, may hold values from -4 to 4
- timestep: int32 [2], P('groups'), parts along dimension 0, may hold values from 0 to 999
- tile_id: int32 [2], P('groups'), parts along dimension 0, may hold values from 0 to 63
- tile_table: float32 [64, 1280], replicated, may hold values from -4 to 4
- null_embed: float32 [2560], P('groups'), parts along dimension 0, may hold values from -4 to 4
- embed_weight: bfloat16 [1280, 640], replicated, may hold values from -0.15625 to 0.15625
- conv_weight: bfloat16 [3, 3, 640, 640], replicated, may hold values from -0.078125 to 0.078125
Outputs:
- noise_pred: bfloat16 [256, 64, 640], P(('groups', 'rows')), parts along dimension 0
- loss: float32 [2], P('groups'), parts along dimension 0
- new_null: float32 [2560], P('groups'), parts along dimension 0
The draws below stay inside these ranges and needn't reach their ends.
There are 2 independent parts, one for each index of `groups`. The reference program is written for one: setup_inputs(seed, part) draws one part's arguments, and reference() takes and returns one part's arrays. A program takes and returns all parts, laid end to end along the dimension named above; an argument that names none is the same for every part. Nothing has to cross between parts.
Inputs may be any that keep to these rules, and one draw needn't show every extreme that they name: `conv_hidden`: first convolution's output, rows and channels of unlike scales.
All inputs are finite; a program needn't handle non-finite values.
Results may differ from the reference program's by a relative error of at most 0.0006.
The reference program's roundings to bfloat16 on the way (of `act_embed`, `act_field` and `cotangent`) count: a program that leaves them out, or rounds other values in their place, can miss the bound.
Values may be sent and summed in bfloat16 or wider, within the bound.
A program may use at most 64 MiB of HBM per device.

```python
import math
import jax
import jax.numpy as jnp
from jax import lax

C = 640
E = 1280
GROUPS = 32
TILES = 64
CW = 64
NR = 128


def draw_conv_hidden(key, part):
    sub_keys = jax.random.split(key, 3)
    row_pos = jnp.arange(NR, dtype=jnp.float32) / (NR - 1)
    row_scale = jnp.exp(math.log(3.0) * row_pos + math.log(4.0) * jax.random.uniform(sub_keys[0], (NR,), jnp.float32))
    chan_scale = jnp.exp(math.log(3.0) * jax.random.uniform(sub_keys[1], (C,), jnp.float32))
    base_draw = jnp.clip(jax.random.normal(sub_keys[2], (NR, CW, C), jnp.float32), -3.0, 3.0)
    return (base_draw * row_scale[:, None, None] * chan_scale).astype(jnp.bfloat16)


def level_of(own_key, extent, pieces, least, largest):
    level = 1.0
    for position, shards_of in pieces:
        draws = jax.random.uniform(jax.random.fold_in(jax.random.fold_in(own_key, 6), position), (shards_of,), jnp.float32, least / len(pieces), largest / len(pieces))
        level = level * jnp.repeat(jnp.exp(draws), extent[position] // shards_of).reshape((-1,) + (1,) * (len(extent) - 1 - position))
    return level


def centred(rng, dims, deviation, bound, cuts=(), kind=jnp.bfloat16):
    entries = deviation * jax.random.normal(rng, dims, jnp.float32)
    if cuts:
        entries = entries * level_of(rng, dims, cuts, -0.22, 0.18)
    return jnp.clip(entries, -bound, bound).astype(kind)


def setup_inputs(seed: int = 0, part: int = 0) -> dict:
    keys = jax.random.split(jax.random.key(seed), 10)
    own_keys = jax.random.split(jax.random.fold_in(keys[9], part), 10)
    return {
        "skip_input": centred(own_keys[0], (NR, CW, C), 1.0, 4.0, ((0, 16),)),
        "conv_hidden": draw_conv_hidden(jax.random.fold_in(jax.random.fold_in(keys[9], part), 71), part),
        "noise_target": centred(own_keys[2], (NR, CW, C), 1.0, 4.0, ((0, 16),)),
        "timestep": jax.random.randint(own_keys[3], (1,), 0, 1000).astype(jnp.int32),
        "tile_id": jax.random.randint(own_keys[4], (1,), 0, TILES).astype(jnp.int32),
        "tile_table": centred(keys[5], (TILES, E), 1.0, 4.0, (), jnp.float32),
        "null_embed": centred(own_keys[6], (E,), 1.0, 4.0, (), jnp.float32),
        "embed_weight": centred(keys[7], (E, C), E ** -0.5, 0.15625),
        "conv_weight": centred(keys[8], (3, 3, C, C), (9 * C) ** -0.5, 0.078125),
    }


def convolve_full(field_in, kernel):
    conv_sum = lax.conv_general_dilated(field_in.astype(jnp.float32)[None], kernel.astype(jnp.float32), (1, 1), ((1, 1), (1, 1)), dimension_numbers=('NHWC', 'HWIO', 'NHWC'), precision=lax.Precision.HIGHEST)
    return conv_sum[0]

def silu_slope(inputs):
    sigmoid_value = jax.nn.sigmoid(inputs)
    return sigmoid_value * (1.0 + inputs * (1.0 - sigmoid_value))

def group_total(chan_sums, group_width):
    return jnp.repeat(lax.optimization_barrier(jnp.sum(chan_sums.reshape(GROUPS, group_width), axis=1)), group_width)

def reference(skip_input, conv_hidden, noise_target, timestep, tile_id, tile_table, null_embed, embed_weight, conv_weight):
    half_width = E // 2
    freq_index = jnp.arange(half_width, dtype=jnp.float32)
    freqs = jnp.exp(-math.log(10000.0) * freq_index / half_width)
    phase_arg = timestep.astype(jnp.float32)[0] * freqs
    time_embed = jnp.concatenate([jnp.cos(phase_arg), jnp.sin(phase_arg)])
    tile_match = jnp.arange(TILES, dtype=jnp.int32) == tile_id[0]
    picked = lax.optimization_barrier(jnp.sum(jnp.where(tile_match[:, None], tile_table, 0.0), axis=0))
    pre_embed = null_embed + time_embed + picked
    act_embed = jax.nn.silu(pre_embed).astype(jnp.bfloat16)
    embed_proj = jnp.dot(act_embed[None, :], embed_weight, preferred_element_type=jnp.float32)[0]
    hidden = conv_hidden.astype(jnp.float32) + embed_proj
    group_width = C // GROUPS
    group_count = NR * CW * group_width
    group_mean = group_total(lax.optimization_barrier(jnp.sum(hidden, axis=(0, 1))), group_width) / group_count
    centered = hidden - group_mean
    group_var = group_total(lax.optimization_barrier(jnp.sum(centered * centered, axis=(0, 1))), group_width) / group_count
    inv_std = 1.0 / jnp.sqrt(group_var + 1e-05)
    normed = centered * inv_std
    act_field = jax.nn.silu(normed).astype(jnp.bfloat16)
    noise_pred = (skip_input.astype(jnp.float32) + convolve_full(act_field, conv_weight)).astype(jnp.bfloat16)
    error_field = noise_pred.astype(jnp.float32) - noise_target.astype(jnp.float32)
    loss = jnp.sum(error_field * error_field) / (NR * CW * C)
    cotangent = error_field.astype(jnp.bfloat16)
    back_kernel = jnp.transpose(jnp.flip(conv_weight, (0, 1)), (0, 1, 3, 2))
    grad_act = convolve_full(cotangent, back_kernel)
    grad_norm = grad_act * silu_slope(normed)
    mean_grad = group_total(lax.optimization_barrier(jnp.sum(grad_norm, axis=(0, 1))), group_width) / group_count
    mean_cross = group_total(lax.optimization_barrier(jnp.sum(grad_norm * normed, axis=(0, 1))), group_width) / group_count
    grad_proj = lax.optimization_barrier(jnp.sum((grad_norm - mean_grad - normed * mean_cross) * inv_std, axis=(0, 1)))
    grad_null = jnp.dot(embed_weight.astype(jnp.float32), grad_proj, precision=lax.Precision.HIGHEST) * silu_slope(pre_embed)
    new_null = null_embed - 0.5 * grad_null / jnp.sqrt(jnp.mean(grad_null * grad_null) + 1e-06)
    return (noise_pred, loss[None], new_null)
```

```python
import functools
import math

import jax
import jax.numpy as jnp
from jax import lax
from jax.experimental import pallas as pl
from jax.experimental.pallas import tpu as pltpu
from jax.sharding import PartitionSpec as P

GROUPS = 32
MESH = pl.DeviceIdType.MESH
F32 = jnp.float32
BF16 = jnp.bfloat16


def pieces(rows):
    out = []
    for row in rows:
        for _ in range(3):
            part = row.astype(BF16).astype(F32)
            out.append(part)
            row = row - part
    height = 16
    index = lax.broadcasted_iota(jnp.int32, (height, rows[0].shape[1]), 0)
    block = jnp.zeros((height, rows[0].shape[1]), F32)
    for place, part in enumerate(out):
        block = jnp.where(index == place, part, block)
    return block.astype(BF16)


def joined(product, count):
    return [
        product[3 * k : 3 * k + 1] + product[3 * k + 1 : 3 * k + 2] + product[3 * k + 2 : 3 * k + 3]
        for k in range(count)
    ]


def group_sums(rows, same_ref):
    product = jnp.dot(pieces(rows), same_ref[...], preferred_element_type=F32)
    return joined(product, len(rows))


def tiles_of(extent, width):
    return [(start, min(width, extent - start)) for start in range(0, extent, width)]


def kernel(
    n, columns,
    time_ref, tile_ref, hidden_hbm, skip_hbm, target_hbm, conv_hbm, embed_hbm, table_ref, null_ref,
    pred_hbm, loss_ref, new_ref,
    hidden, skip, target, conv, embed, field, cot, pred, normed, slope, edge_send, edge_low, edge_high,
    hid_low, hid_high, same, stat_send, stat_recv, grad_send, grad_recv,
    load_sem, stat_ssem, stat_rsem, grad_ssem, grad_rsem, halo_ssem, halo_rsem, cot_ssem, cot_rsem,
):
    me = lax.axis_index("rows")
    cells, channels = hidden.shape
    group_width = channels // GROUPS
    half = null_ref.shape[1] // 2
    has_low, has_high = me > 0, me < n - 1

    barrier = pltpu.get_barrier_semaphore()
    for k in range(1, n):
        pl.semaphore_signal(barrier, inc=1, device_id={"rows": lax.rem(me + k, n)}, device_id_type=MESH)

    loads = []
    for place, (src, dst) in enumerate(
        ((hidden_hbm, hidden), (embed_hbm, embed), (conv_hbm, conv), (skip_hbm, skip), (target_hbm, target))
    ):
        copy = pltpu.make_async_copy(src, dst, load_sem.at[place])
        copy.start()
        loads.append(copy)
    loads[0].wait()

    raw = hidden[...].astype(F32)
    chan_sum = jnp.sum(raw, axis=0, keepdims=True)
    spread = raw - chan_sum * (1.0 / cells)
    chan_sq = jnp.sum(spread * spread, axis=0, keepdims=True)
    stat_send[:, :channels] = chan_sum
    stat_send[:, channels:] = chan_sq

    pl.semaphore_wait(barrier, n - 1)

    def send_all(src, recv, ssem, rsem):
        copies = []
        for k in range(1, n):
            copy = pltpu.make_async_remote_copy(
                src_ref=src, dst_ref=recv.at[me], send_sem=ssem.at[k], recv_sem=rsem.at[me],
                device_id={"rows": lax.rem(me + k, n)}, device_id_type=MESH,
            )
            copy.start()
            copies.append(copy)
        return copies

    def wait_all(copies, src, recv, ssem, rsem):
        for k in range(1, n):
            sender = lax.rem(me + k, n)
            pltpu.make_async_remote_copy(
                src_ref=src, dst_ref=recv.at[sender], send_sem=ssem.at[k], recv_sem=rsem.at[sender],
                device_id={"rows": sender}, device_id_type=MESH,
            ).wait_recv()

    stat_copies = send_all(stat_send, stat_recv, stat_ssem, stat_rsem)
    stat_recv[me] = stat_send[...]

    def halo_copies(low_src, high_src, low_dst, high_dst, ssem, rsem):
        down = pltpu.make_async_remote_copy(
            src_ref=low_src, dst_ref=high_dst, send_sem=ssem.at[0], recv_sem=rsem.at[0],
            device_id={"rows": lax.rem(me + n - 1, n)}, device_id_type=MESH,
        )
        up = pltpu.make_async_remote_copy(
            src_ref=high_src, dst_ref=low_dst, send_sem=ssem.at[1], recv_sem=rsem.at[1],
            device_id={"rows": lax.rem(me + 1, n)}, device_id_type=MESH,
        )
        return down, up

    raw_halo = halo_copies(
        hidden.at[pl.ds(0, columns)], hidden.at[pl.ds(cells - columns, columns)],
        hid_low, hid_high, halo_ssem, halo_rsem,
    )
    for copy in raw_halo:
        copy.start()

    index = lax.broadcasted_iota(jnp.int32, (1, half), 1).astype(F32)
    freqs = jnp.exp(-math.log(10000.0) * index / half)
    phase = time_ref[0].astype(F32) * freqs
    tile_row = lax.broadcasted_iota(jnp.int32, table_ref.shape, 0)
    picked = jnp.sum(jnp.where(tile_row == tile_ref[0], table_ref[...], 0.0), axis=0, keepdims=True)
    pre_embed = null_ref[...] + jnp.concatenate([jnp.cos(phase), jnp.sin(phase)], axis=1) + picked
    embed_sig = jax.nn.sigmoid(pre_embed)
    act_embed = jnp.broadcast_to((pre_embed * embed_sig), (16, 2 * half)).astype(BF16)
    loads[1].wait()
    proj = jnp.dot(act_embed, embed[...], preferred_element_type=F32)[0:1]
    embed_slope = embed_sig * (1.0 + pre_embed * (1.0 - embed_sig))

    row_group = jnp.floor(
        (lax.broadcasted_iota(jnp.int32, (channels, channels), 0).astype(F32) + 0.5) * (1.0 / group_width)
    )
    col_group = jnp.floor(
        (lax.broadcasted_iota(jnp.int32, (channels, channels), 1).astype(F32) + 0.5) * (1.0 / group_width)
    )
    same[...] = jnp.where(row_group == col_group, 1.0, 0.0).astype(BF16)

    wait_all(stat_copies, stat_send, stat_recv, stat_ssem, stat_rsem)
    all_sums = stat_recv[:, :, :channels]
    total_sum = jnp.sum(all_sums, axis=0)
    grid_cells = cells * n
    group_count = grid_cells * group_width
    chan_mean = total_sum * (1.0 / grid_cells)
    off = all_sums * (1.0 / cells) - chan_mean[None]
    chan_m2 = jnp.sum(stat_recv[:, :, channels:] + cells * (off * off), axis=0)
    hid_mean = chan_mean + proj
    (mean_total,) = group_sums([hid_mean], same)
    group_mean = mean_total * (1.0 / group_width)
    shift = hid_mean - group_mean
    (var_total,) = group_sums([chan_m2 + grid_cells * (shift * shift)], same)
    group_var = var_total * (1.0 / group_count)
    inv_std = 1.0 / jnp.sqrt(group_var + 1e-05)
    normed_sum = shift * inv_std * grid_cells

    col_index = lax.broadcasted_iota(jnp.int32, (columns, channels), 0)

    def spread_columns(block, place, buffer, flip):
        left = jnp.where(col_index == 0, 0.0, pltpu.roll(block, 1, 0))
        right = jnp.where(col_index == columns - 1, 0.0, pltpu.roll(block, columns - 1, 0))
        if flip:
            left, right = right, left
        for b, part in enumerate((left, block, right)):
            buffer[pl.ds(place, columns), b * channels : (b + 1) * channels] = part.astype(BF16)

    def normalised(block):
        return ((block.astype(F32) + proj) - group_mean) * inv_std

    def own_row(r, carry):
        place = pl.multiple_of(r * columns, columns)
        value = normalised(hidden[pl.ds(place, columns), :])
        sig = jax.nn.sigmoid(value)
        normed[pl.ds(place, columns), :] = value
        slope[pl.ds(place, columns), :] = sig * (1.0 + value * (1.0 - sig))
        spread_columns(value * sig, pl.multiple_of(place + columns, columns), field, False)
        return carry

    lax.fori_loop(0, cells // columns, own_row, 0)

    raw_halo[0].wait()
    raw_halo[1].wait()
    for ref, place, inside in ((hid_low, 0, has_low), (hid_high, cells + columns, has_high)):
        value = normalised(ref[...])
        active = jnp.where(inside, value * jax.nn.sigmoid(value), 0.0)
        spread_columns(active, place, field, False)

    loads[2].wait()
    loads[3].wait()
    loads[4].wait()
    depth = 3 * channels
    loss_part = jnp.zeros((1, 1), F32)
    for start, width in tiles_of(channels, 256):
        acc = None
        for a in range(3):
            part = jnp.dot(
                field[a * columns : a * columns + cells, :],
                conv[a * depth : (a + 1) * depth, start : start + width],
                preferred_element_type=F32,
            )
            acc = part if acc is None else acc + part
        out = (skip[:, start : start + width].astype(F32) + acc).astype(BF16)
        pred[:, start : start + width] = out
        error = out.astype(F32) - target[:, start : start + width].astype(F32)
        loss_part = loss_part + jnp.sum(error * error, keepdims=True)
        rounded = error.astype(BF16)
        skip[:, start : start + width] = rounded
        edge_send[0, :, start : start + width] = rounded[:columns]
        edge_send[1, :, start : start + width] = rounded[cells - columns :]

    cot_halo = halo_copies(edge_send.at[0], edge_send.at[1], edge_low, edge_high, cot_ssem, cot_rsem)
    for copy in cot_halo:
        copy.start()
    pred_copy = pltpu.make_async_copy(pred, pred_hbm, load_sem.at[5])
    pred_copy.start()

    def cot_row(r, carry):
        place = pl.multiple_of(r * columns, columns)
        block = skip[pl.ds(place, columns), :].astype(F32)
        spread_columns(block, pl.multiple_of(place + columns, columns), cot, True)
        return carry

    lax.fori_loop(0, cells // columns, cot_row, 0)
    cot_halo[0].wait()
    cot_halo[1].wait()
    for ref, place, inside in ((edge_low, 0, has_low), (edge_high, cells + columns, has_high)):
        spread_columns(jnp.where(inside, ref[...].astype(F32), 0.0), place, cot, True)

    for start, width in tiles_of(channels, 256):
        acc = None
        for a in (1, 0, 2):
            for b in range(3):
                base = (a * 3 + b) * channels + start
                part = lax.dot_general(
                    cot[(2 - a) * columns : (2 - a) * columns + cells, b * channels : (b + 1) * channels],
                    conv[base : base + width, :],
                    (((1,), (1,)), ((), ())),
                    preferred_element_type=F32,
                )
                acc = part if acc is None else acc + part
        grad = acc * slope[:, start : start + width]
        cross = grad * normed[:, start : start + width]
        grad_send[:, start : start + width] = jnp.sum(grad, axis=0, keepdims=True)
        grad_send[:, channels + start : channels + start + width] = jnp.sum(cross, axis=0, keepdims=True)
    grad_send[:, 2 * channels :] = jnp.broadcast_to(loss_part, (1, 128))

    grad_copies = send_all(grad_send, grad_recv, grad_ssem, grad_rsem)
    grad_recv[me] = grad_send[...]
    wait_all(grad_copies, grad_send, grad_recv, grad_ssem, grad_rsem)
    totals = jnp.sum(grad_recv[...], axis=0)
    grad_chan = totals[:, :channels]
    grad_groups, cross_groups = group_sums([grad_chan, totals[:, channels : 2 * channels]], same)
    mean_grad = grad_groups * (1.0 / group_count)
    mean_cross = cross_groups * (1.0 / group_count)
    grad_proj = (grad_chan - mean_grad * grid_cells - mean_cross * normed_sum) * inv_std
    loss_ref[...] = totals[:, 2 * channels : 2 * channels + 1] * (1.0 / (grid_cells * channels))
    back = lax.dot_general(
        pieces([grad_proj]), embed[...], (((1,), (1,)), ((), ())), preferred_element_type=F32
    )
    grad_null = joined(back, 1)[0] * embed_slope
    scale = 0.5 / jnp.sqrt(jnp.sum(grad_null * grad_null, keepdims=True) * (1.0 / (2 * half)) + 1e-06)
    new_ref[...] = null_ref[...] - grad_null * scale

    pred_copy.wait()
    for copy in stat_copies + grad_copies:
        copy.wait_send()


def body(n, skip_input, conv_hidden, noise_target, timestep, tile_id, tile_table, null_embed, embed_weight, conv_weight):
    rows_local, columns, channels = skip_input.shape
    cells = rows_local * columns
    width = null_embed.shape[0]
    any_spec = pl.BlockSpec(memory_space=pl.ANY)
    vmem = pl.BlockSpec(memory_space=pltpu.VMEM)
    smem = pl.BlockSpec(memory_space=pltpu.SMEM)
    dma = pltpu.SemaphoreType.DMA
    padded = cells + 2 * columns
    pred, loss, new_null = pl.pallas_call(
        functools.partial(kernel, n, columns),
        out_shape=(
            jax.ShapeDtypeStruct((cells, channels), BF16),
            jax.ShapeDtypeStruct((1, 1), F32),
            jax.ShapeDtypeStruct((1, width), F32),
        ),
        in_specs=[smem, smem] + [any_spec] * 5 + [vmem, vmem],
        out_specs=(any_spec, vmem, vmem),
        scratch_shapes=[
            pltpu.VMEM((cells, channels), BF16),
            pltpu.VMEM((cells, channels), BF16),
            pltpu.VMEM((cells, channels), BF16),
            pltpu.VMEM((9 * channels, channels), BF16),
            pltpu.VMEM((width, channels), BF16),
            pltpu.VMEM((padded, 3 * channels), BF16),
            pltpu.VMEM((padded, 3 * channels), BF16),
            pltpu.VMEM((cells, channels), BF16),
            pltpu.VMEM((cells, channels), F32),
            pltpu.VMEM((cells, channels), F32),
            pltpu.VMEM((2, columns, channels), BF16),
            pltpu.VMEM((columns, channels), BF16),
            pltpu.VMEM((columns, channels), BF16),
            pltpu.VMEM((columns, channels), BF16),
            pltpu.VMEM((columns, channels), BF16),
            pltpu.VMEM((channels, channels), BF16),
            pltpu.VMEM((1, 2 * channels), F32),
            pltpu.VMEM((n, 1, 2 * channels), F32),
            pltpu.VMEM((1, 2 * channels + 128), F32),
            pltpu.VMEM((n, 1, 2 * channels + 128), F32),
            dma((6,)), dma((n,)), dma((n,)), dma((n,)), dma((n,)), dma((2,)), dma((2,)), dma((2,)), dma((2,)),
        ],
        compiler_params=pltpu.CompilerParams(
            collective_id=0, has_side_effects=True, vmem_limit_bytes=56 * 1024 * 1024
        ),
        name="resblock_step",
    )(
        timestep, tile_id,
        conv_hidden.reshape(cells, channels), skip_input.reshape(cells, channels),
        noise_target.reshape(cells, channels), conv_weight.reshape(9 * channels, channels),
        embed_weight, tile_table, null_embed.reshape(1, width),
    )
    return pred.reshape(rows_local, columns, channels), loss.reshape(1), new_null.reshape(width)


def solution(mesh):
    rows = P(("groups", "rows"), None, None)
    in_specs = (rows, rows, rows, P("groups"), P("groups"), P(), P("groups"), P(), P())
    out_specs = (rows, P("groups"), P("groups"))
    return jax.shard_map(
        functools.partial(body, mesh.shape["rows"]),
        mesh=mesh, in_specs=in_specs, out_specs=out_specs, check_vma=False,
    )
```

```python
import functools
import math

import jax
import jax.numpy as jnp
from jax import lax
from jax.experimental import pallas as pl
from jax.experimental.pallas import tpu as pltpu
from jax.sharding import PartitionSpec as P

GROUPS = 32
MESH = pl.DeviceIdType.MESH
F32 = jnp.float32
BF16 = jnp.bfloat16


def pieces(rows):
    out = []
    for row in rows:
        for _ in range(3):
            part = row.astype(BF16).astype(F32)
            out.append(part)
            row = row - part
    height = 16
    index = lax.broadcasted_iota(jnp.int32, (height, rows[0].shape[1]), 0)
    block = jnp.zeros((height, rows[0].shape[1]), F32)
    for place, part in enumerate(out):
        block = jnp.where(index == place, part, block)
    return block.astype(BF16)


def joined(product, count):
    return [
        product[3 * k : 3 * k + 1] + product[3 * k + 1 : 3 * k + 2] + product[3 * k + 2 : 3 * k + 3]
        for k in range(count)
    ]


def group_sums(rows, same_ref):
    product = jnp.dot(pieces(rows), same_ref[...], preferred_element_type=F32)
    return joined(product, len(rows))


def tiles_of(extent, width):
    return [(start, min(width, extent - start)) for start in range(0, extent, width)]


def kernel(
    n, columns,
    time_ref, tile_ref, hidden_hbm, skip_hbm, target_hbm, conv_hbm, embed_hbm, table_hbm, null_hbm,
    pred, embed, proj_out, loss_out, null_out, slope_out,
    hidden, skip, target, conv, table_ref, null_ref, field, cot, normed, edge_send, edge_low, edge_high,
    hid_low, hid_high, same, stat_send, stat_recv, grad_send, grad_recv,
    load_sem, stat_ssem, stat_rsem, grad_ssem, grad_rsem, halo_ssem, halo_rsem, cot_ssem, cot_rsem,
):
    me = lax.axis_index("rows")
    cells, channels = hidden.shape
    group_width = channels // GROUPS
    half = null_ref.shape[0] // 2
    has_low, has_high = me > 0, me < n - 1

    barrier = pltpu.get_barrier_semaphore()
    for k in range(1, n):
        pl.semaphore_signal(barrier, inc=1, device_id={"rows": lax.rem(me + k, n)}, device_id_type=MESH)

    loads = []
    for place, (src, dst) in enumerate(
        (
            (hidden_hbm, hidden), (null_hbm, null_ref),
            (table_hbm, table_ref), (embed_hbm, embed), (conv_hbm, conv), (skip_hbm, skip), (target_hbm, target),
        )
    ):
        copy = pltpu.make_async_copy(src, dst, load_sem.at[place])
        copy.start()
        loads.append(copy)
    loads[0].wait()

    raw = hidden[...].astype(F32)
    chan_sum = jnp.sum(raw, axis=0, keepdims=True)
    spread = raw - chan_sum * (1.0 / cells)
    chan_sq = jnp.sum(spread * spread, axis=0, keepdims=True)
    stat_send[:, :channels] = chan_sum
    stat_send[:, channels:] = chan_sq

    pl.semaphore_wait(barrier, n - 1)

    def send_all(src, recv, ssem, rsem):
        copies = []
        for k in range(1, n):
            copy = pltpu.make_async_remote_copy(
                src_ref=src, dst_ref=recv.at[me], send_sem=ssem.at[k], recv_sem=rsem.at[me],
                device_id={"rows": lax.rem(me + k, n)}, device_id_type=MESH,
            )
            copy.start()
            copies.append(copy)
        return copies

    def wait_all(copies, src, recv, ssem, rsem):
        for k in range(1, n):
            sender = lax.rem(me + k, n)
            pltpu.make_async_remote_copy(
                src_ref=src, dst_ref=recv.at[sender], send_sem=ssem.at[k], recv_sem=rsem.at[sender],
                device_id={"rows": sender}, device_id_type=MESH,
            ).wait_recv()

    stat_copies = send_all(stat_send, stat_recv, stat_ssem, stat_rsem)
    stat_recv[me] = stat_send[...]

    def halo_copies(low_src, high_src, low_dst, high_dst, ssem, rsem):
        down = pltpu.make_async_remote_copy(
            src_ref=low_src, dst_ref=high_dst, send_sem=ssem.at[0], recv_sem=rsem.at[0],
            device_id={"rows": lax.rem(me + n - 1, n)}, device_id_type=MESH,
        )
        up = pltpu.make_async_remote_copy(
            src_ref=high_src, dst_ref=low_dst, send_sem=ssem.at[1], recv_sem=rsem.at[1],
            device_id={"rows": lax.rem(me + 1, n)}, device_id_type=MESH,
        )
        return down, up

    def start_halo(pair):
        pl.when(has_low)(pair[0].start)
        pl.when(has_high)(pair[1].start)

    def wait_halo(pair):
        pl.when(has_low)(pair[0].wait_send)
        pl.when(has_high)(pair[1].wait_send)
        pl.when(has_high)(pair[0].wait_recv)
        pl.when(has_low)(pair[1].wait_recv)

    raw_halo = halo_copies(
        hidden.at[pl.ds(0, columns)], hidden.at[pl.ds(cells - columns, columns)],
        hid_low, hid_high, halo_ssem, halo_rsem,
    )
    start_halo(raw_halo)

    index = lax.broadcasted_iota(jnp.int32, (1, half), 1).astype(F32)
    freqs = jnp.exp(-math.log(10000.0) * index / half)
    for copy in loads[1:3]:
        copy.wait()
    null_row = null_ref[...].reshape(1, 2 * half)
    phase = time_ref[0].astype(F32) * freqs
    tile_row = lax.broadcasted_iota(jnp.int32, table_ref.shape, 0)
    picked = jnp.sum(jnp.where(tile_row == tile_ref[0], table_ref[...], 0.0), axis=0, keepdims=True)
    pre_embed = null_row + jnp.concatenate([jnp.cos(phase), jnp.sin(phase)], axis=1) + picked
    embed_sig = jax.nn.sigmoid(pre_embed)
    act_embed = jnp.broadcast_to((pre_embed * embed_sig), (16, 2 * half)).astype(BF16)
    loads[3].wait()
    proj = jnp.dot(act_embed, embed[...], preferred_element_type=F32)[0:1]
    null_out[...] = null_row
    slope_out[...] = embed_sig * (1.0 + pre_embed * (1.0 - embed_sig))

    row_group = jnp.floor(
        (lax.broadcasted_iota(jnp.int32, (channels, channels), 0).astype(F32) + 0.5) * (1.0 / group_width)
    )
    col_group = jnp.floor(
        (lax.broadcasted_iota(jnp.int32, (channels, channels), 1).astype(F32) + 0.5) * (1.0 / group_width)
    )
    same[...] = jnp.where(row_group == col_group, 1.0, 0.0).astype(BF16)

    wait_all(stat_copies, stat_send, stat_recv, stat_ssem, stat_rsem)
    all_sums = stat_recv[:, :, :channels]
    total_sum = jnp.sum(all_sums, axis=0)
    grid_cells = cells * n
    group_count = grid_cells * group_width
    chan_mean = total_sum * (1.0 / grid_cells)
    off = all_sums * (1.0 / cells) - chan_mean[None]
    chan_m2 = jnp.sum(stat_recv[:, :, channels:] + cells * (off * off), axis=0)
    hid_mean = chan_mean + proj
    (mean_total,) = group_sums([hid_mean], same)
    group_mean = mean_total * (1.0 / group_width)
    shift = hid_mean - group_mean
    (var_total,) = group_sums([chan_m2 + grid_cells * (shift * shift)], same)
    group_var = var_total * (1.0 / group_count)
    inv_std = 1.0 / jnp.sqrt(group_var + 1e-05)
    normed_sum = shift * inv_std * grid_cells

    col_index = lax.broadcasted_iota(jnp.int32, (columns, channels), 0)

    def spread_columns(block, place, buffer, flip):
        left = jnp.where(col_index == 0, 0.0, pltpu.roll(block, 1, 0))
        right = jnp.where(col_index == columns - 1, 0.0, pltpu.roll(block, columns - 1, 0))
        if flip:
            left, right = right, left
        for b, part in enumerate((left, block, right)):
            buffer[pl.ds(place, columns), b * channels : (b + 1) * channels] = part.astype(BF16)

    def normalised(block):
        return ((block.astype(F32) + proj) - group_mean) * inv_std

    def own_row(r, carry):
        place = pl.multiple_of(r * columns, columns)
        value = normalised(hidden[pl.ds(place, columns), :])
        sig = jax.nn.sigmoid(value)
        normed[pl.ds(place, columns), :] = value
        spread_columns(value * sig, pl.multiple_of(place + columns, columns), field, False)
        return carry

    lax.fori_loop(0, cells // columns, own_row, 0)

    wait_halo(raw_halo)

    def outside(place, buffer):
        buffer[pl.ds(place, columns), :] = jnp.zeros((columns, 3 * channels), BF16)

    for ref, place, inside in ((hid_low, 0, has_low), (hid_high, cells + columns, has_high)):

        @pl.when(inside)
        def _():
            value = normalised(ref[...])
            spread_columns(value * jax.nn.sigmoid(value), place, field, False)

        pl.when(jnp.logical_not(inside))(functools.partial(outside, place, field))

    for copy in loads[4:]:
        copy.wait()
    col_tall = lax.rem(lax.broadcasted_iota(jnp.int32, (cells, 256), 0), columns)
    depth = 3 * channels
    loss_part = jnp.zeros((1, 1), F32)
    for start, width in tiles_of(channels, 256):
        acc = None
        for a in range(3):
            part = jnp.dot(
                field[a * columns : a * columns + cells, :],
                conv[a * depth : (a + 1) * depth, start : start + width],
                preferred_element_type=F32,
            )
            acc = part if acc is None else acc + part
        out = (skip[:, start : start + width].astype(F32) + acc).astype(BF16)
        pred[:, start : start + width] = out
        error = out.astype(F32) - target[:, start : start + width].astype(F32)
        loss_part = loss_part + jnp.sum(error * error, keepdims=True)
        rounded = error.astype(BF16)
        wide = rounded.astype(F32)
        near = col_tall[:, :width]
        after = jnp.where(near == columns - 1, 0.0, pltpu.roll(wide, cells - 1, 0)).astype(BF16)
        before = jnp.where(near == 0, 0.0, pltpu.roll(wide, 1, 0)).astype(BF16)
        for b, part in enumerate((after, rounded, before)):
            cot[columns : columns + cells, b * channels + start : b * channels + start + width] = part
        edge_send[0, :, start : start + width] = rounded[:columns]
        edge_send[1, :, start : start + width] = rounded[cells - columns :]

    cot_halo = halo_copies(edge_send.at[0], edge_send.at[1], edge_low, edge_high, cot_ssem, cot_rsem)
    start_halo(cot_halo)
    wait_halo(cot_halo)
    for ref, place, inside in ((edge_low, 0, has_low), (edge_high, cells + columns, has_high)):

        @pl.when(inside)
        def _():
            spread_columns(ref[...].astype(F32), place, cot, True)

        pl.when(jnp.logical_not(inside))(functools.partial(outside, place, cot))

    for start, width in tiles_of(channels, 256):
        acc = None
        for a in (1, 0, 2):
            for b in range(3):
                base = (a * 3 + b) * channels + start
                part = lax.dot_general(
                    cot[(2 - a) * columns : (2 - a) * columns + cells, b * channels : (b + 1) * channels],
                    conv[base : base + width, :],
                    (((1,), (1,)), ((), ())),
                    preferred_element_type=F32,
                )
                acc = part if acc is None else acc + part
        value = normed[:, start : start + width]
        sig = jax.nn.sigmoid(value)
        grad = acc * (sig * (1.0 + value * (1.0 - sig)))
        cross = grad * value
        grad_send[:, start : start + width] = jnp.sum(grad, axis=0, keepdims=True)
        grad_send[:, channels + start : channels + start + width] = jnp.sum(cross, axis=0, keepdims=True)
    grad_send[:, 2 * channels :] = jnp.broadcast_to(loss_part, (1, 128))

    grad_copies = send_all(grad_send, grad_recv, grad_ssem, grad_rsem)
    grad_recv[me] = grad_send[...]
    wait_all(grad_copies, grad_send, grad_recv, grad_ssem, grad_rsem)
    totals = jnp.sum(grad_recv[...], axis=0)
    grad_chan = totals[:, :channels]
    grad_groups, cross_groups = group_sums([grad_chan, totals[:, channels : 2 * channels]], same)
    mean_grad = grad_groups * (1.0 / group_count)
    mean_cross = cross_groups * (1.0 / group_count)
    grad_proj = (grad_chan - mean_grad * grid_cells - mean_cross * normed_sum) * inv_std
    proj_out[...] = grad_proj
    loss_out[...] = totals[:, 2 * channels :] * (1.0 / (grid_cells * channels))
    for copy in stat_copies + grad_copies:
        copy.wait_send()


def finish(pred_ref, embed_ref, proj_ref, loss_in, null_ref, slope_ref, pred_hbm, loss_ref, new_ref, sem):
    copy = pltpu.make_async_copy(pred_ref, pred_hbm, sem)
    copy.start()
    back = lax.dot_general(
        pieces([proj_ref[...]]), embed_ref[...], (((1,), (1,)), ((), ())), preferred_element_type=F32
    )
    grad_null = joined(back, 1)[0] * slope_ref[...]
    width = grad_null.shape[1]
    scale = 0.5 / jnp.sqrt(jnp.sum(grad_null * grad_null, keepdims=True) * (1.0 / width) + 1e-06)
    new_ref[...] = (null_ref[...] - grad_null * scale).reshape(width)
    loss_ref[...] = jnp.sum(loss_in[:, :1], axis=1)
    copy.wait()


def body(n, skip_input, conv_hidden, noise_target, timestep, tile_id, tile_table, null_embed, embed_weight, conv_weight):
    rows_local, columns, channels = skip_input.shape
    cells = rows_local * columns
    width = null_embed.shape[0]
    any_spec = pl.BlockSpec(memory_space=pl.ANY)
    vmem = pl.BlockSpec(memory_space=pltpu.VMEM)
    smem = pl.BlockSpec(memory_space=pltpu.SMEM)
    dma = pltpu.SemaphoreType.DMA
    padded = cells + 2 * columns
    held = pl.pallas_call(
        functools.partial(kernel, n, columns),
        out_shape=(
            pltpu.VMEM((cells, channels), BF16),
            pltpu.VMEM((width, channels), BF16),
            pltpu.VMEM((1, channels), F32),
            pltpu.VMEM((1, 128), F32),
            pltpu.VMEM((1, width), F32),
            pltpu.VMEM((1, width), F32),
        ),
        in_specs=[smem] * 2 + [any_spec] * 7,
        out_specs=(vmem,) * 6,
        scratch_shapes=[
            pltpu.VMEM((cells, channels), BF16),
            pltpu.VMEM((cells, channels), BF16),
            pltpu.VMEM((cells, channels), BF16),
            pltpu.VMEM((9 * channels, channels), BF16),
            pltpu.VMEM(tile_table.shape, F32),
            pltpu.VMEM((width,), F32),
            pltpu.VMEM((padded, 3 * channels), BF16),
            pltpu.VMEM((padded, 3 * channels), BF16),
            pltpu.VMEM((cells, channels), F32),
            pltpu.VMEM((2, columns, channels), BF16),
            pltpu.VMEM((columns, channels), BF16),
            pltpu.VMEM((columns, channels), BF16),
            pltpu.VMEM((columns, channels), BF16),
            pltpu.VMEM((columns, channels), BF16),
            pltpu.VMEM((channels, channels), BF16),
            pltpu.VMEM((1, 2 * channels), F32),
            pltpu.VMEM((n, 1, 2 * channels), F32),
            pltpu.VMEM((1, 2 * channels + 128), F32),
            pltpu.VMEM((n, 1, 2 * channels + 128), F32),
            dma((7,)), dma((n,)), dma((n,)), dma((n,)), dma((n,)), dma((2,)), dma((2,)), dma((2,)), dma((2,)),
        ],
        compiler_params=pltpu.CompilerParams(
            collective_id=0, has_side_effects=True, vmem_limit_bytes=40 * 1024 * 1024
        ),
        name="resblock_step",
    )(timestep, tile_id, *[pltpu.with_memory_space_constraint(part, pltpu.HBM) for part in (
        conv_hidden.reshape(cells, channels), skip_input.reshape(cells, channels),
        noise_target.reshape(cells, channels), conv_weight.reshape(9 * channels, channels),
        embed_weight, tile_table, null_embed,
    )])
    held = [pltpu.with_memory_space_constraint(part, pltpu.VMEM) for part in held]
    pred, loss, new_null = pl.pallas_call(
        finish,
        out_shape=(
            jax.ShapeDtypeStruct((cells, channels), BF16),
            jax.ShapeDtypeStruct((1,), F32),
            jax.ShapeDtypeStruct((width,), F32),
        ),
        in_specs=[vmem] * 6,
        out_specs=(any_spec, vmem, vmem),
        scratch_shapes=[dma],
        compiler_params=pltpu.CompilerParams(vmem_limit_bytes=16 * 1024 * 1024),
        name="resblock_finish",
    )(*held)
    return pred.reshape(rows_local, columns, channels), loss, new_null


def solution(mesh):
    rows = P(("groups", "rows"), None, None)
    in_specs = (rows, rows, rows, P("groups"), P("groups"), P(), P("groups"), P(), P())
    out_specs = (rows, P("groups"), P("groups"))
    return jax.shard_map(
        functools.partial(body, mesh.shape["rows"]),
        mesh=mesh, in_specs=in_specs, out_specs=out_specs, check_vma=False,
    )
```

```python
import functools
import math

import jax
import jax.numpy as jnp
from jax import lax
from jax.experimental import pallas as pl
from jax.experimental.pallas import tpu as pltpu
from jax.sharding import PartitionSpec as P

GROUPS = 32
MESH = pl.DeviceIdType.MESH
F32 = jnp.float32
BF16 = jnp.bfloat16


def pieces(rows):
    out = []
    for row in rows:
        for _ in range(3):
            part = row.astype(BF16).astype(F32)
            out.append(part)
            row = row - part
    height = 16
    index = lax.broadcasted_iota(jnp.int32, (height, rows[0].shape[1]), 0)
    block = jnp.zeros((height, rows[0].shape[1]), F32)
    for place, part in enumerate(out):
        block = jnp.where(index == place, part, block)
    return block.astype(BF16)


def joined(product, count):
    return [
        product[3 * k : 3 * k + 1] + product[3 * k + 1 : 3 * k + 2] + product[3 * k + 2 : 3 * k + 3]
        for k in range(count)
    ]


def group_sums(rows, same_ref):
    product = jnp.dot(pieces(rows), same_ref[...], preferred_element_type=F32)
    return joined(product, len(rows))


def tiles_of(extent, width):
    return [(start, min(width, extent - start)) for start in range(0, extent, width)]


def kernel(
    n, columns,
    time_ref, tile_ref, hidden_hbm, skip_hbm, target_hbm, conv_hbm, embed_hbm, table_hbm, null_hbm,
    pred, embed, proj_out, loss_out, null_out, slope_out,
    hidden, skip, target, conv, table_ref, null_ref, field, cot, normed, edge_send, edge_low, edge_high,
    hid_low, hid_high, same, partial, stat_send, stat_recv, head_send, head_recv, tail_send, tail_recv,
    load_sem, stat_ssem, stat_rsem, head_ssem, head_rsem, tail_ssem, tail_rsem, halo_ssem, halo_rsem, cot_ssem, cot_rsem,
):
    me = lax.axis_index("rows")
    cells, channels = hidden.shape
    group_width = channels // GROUPS
    half = null_ref.shape[0] // 2
    has_low, has_high = me > 0, me < n - 1

    barrier = pltpu.get_barrier_semaphore()
    for k in range(1, n):
        pl.semaphore_signal(barrier, inc=1, device_id={"rows": lax.rem(me + k, n)}, device_id_type=MESH)

    loads = []
    for place, (src, dst) in enumerate(
        (
            (hidden_hbm, hidden), (null_hbm, null_ref),
            (table_hbm, table_ref), (embed_hbm, embed), (conv_hbm, conv), (skip_hbm, skip), (target_hbm, target),
        )
    ):
        copy = pltpu.make_async_copy(src, dst, load_sem.at[place])
        copy.start()
        loads.append(copy)
    loads[0].wait()

    raw = hidden[...].astype(F32)
    chan_sum = jnp.sum(raw, axis=0, keepdims=True)
    spread = raw - chan_sum * (1.0 / cells)
    chan_sq = jnp.sum(spread * spread, axis=0, keepdims=True)
    stat_send[:, :channels] = chan_sum
    stat_send[:, channels:] = chan_sq

    pl.semaphore_wait(barrier, n - 1)

    def send_all(src, recv, ssem, rsem):
        copies = []
        for k in range(1, n):
            copy = pltpu.make_async_remote_copy(
                src_ref=src, dst_ref=recv.at[me], send_sem=ssem.at[k], recv_sem=rsem.at[me],
                device_id={"rows": lax.rem(me + k, n)}, device_id_type=MESH,
            )
            copy.start()
            copies.append(copy)
        return copies

    def wait_all(copies, src, recv, ssem, rsem):
        for k in range(1, n):
            sender = lax.rem(me + k, n)
            pltpu.make_async_remote_copy(
                src_ref=src, dst_ref=recv.at[sender], send_sem=ssem.at[k], recv_sem=rsem.at[sender],
                device_id={"rows": sender}, device_id_type=MESH,
            ).wait_recv()

    stat_copies = send_all(stat_send, stat_recv, stat_ssem, stat_rsem)
    stat_recv[me] = stat_send[...]

    def halo_copies(low_src, high_src, low_dst, high_dst, ssem, rsem, place=0):
        down = pltpu.make_async_remote_copy(
            src_ref=low_src, dst_ref=high_dst, send_sem=ssem.at[place], recv_sem=rsem.at[place],
            device_id={"rows": lax.rem(me + n - 1, n)}, device_id_type=MESH,
        )
        up = pltpu.make_async_remote_copy(
            src_ref=high_src, dst_ref=low_dst, send_sem=ssem.at[place + 1], recv_sem=rsem.at[place + 1],
            device_id={"rows": lax.rem(me + 1, n)}, device_id_type=MESH,
        )
        return down, up

    def start_halo(pair):
        pl.when(has_low)(pair[0].start)
        pl.when(has_high)(pair[1].start)

    def wait_halo(pair):
        pl.when(has_low)(pair[0].wait_send)
        pl.when(has_high)(pair[1].wait_send)
        pl.when(has_high)(pair[0].wait_recv)
        pl.when(has_low)(pair[1].wait_recv)

    raw_halo = halo_copies(
        hidden.at[pl.ds(0, columns)], hidden.at[pl.ds(cells - columns, columns)],
        hid_low, hid_high, halo_ssem, halo_rsem,
    )
    start_halo(raw_halo)

    index = lax.broadcasted_iota(jnp.int32, (1, half), 1).astype(F32)
    freqs = jnp.exp(-math.log(10000.0) * index / half)
    for copy in loads[1:3]:
        copy.wait()
    null_row = null_ref[...].reshape(1, 2 * half)
    phase = time_ref[0].astype(F32) * freqs
    tile_row = lax.broadcasted_iota(jnp.int32, table_ref.shape, 0)
    picked = jnp.sum(jnp.where(tile_row == tile_ref[0], table_ref[...], 0.0), axis=0, keepdims=True)
    pre_embed = null_row + jnp.concatenate([jnp.cos(phase), jnp.sin(phase)], axis=1) + picked
    embed_sig = jax.nn.sigmoid(pre_embed)
    act_embed = jnp.broadcast_to((pre_embed * embed_sig), (16, 2 * half)).astype(BF16)
    loads[3].wait()
    proj = jnp.dot(act_embed, embed[...], preferred_element_type=F32)[0:1]
    null_out[...] = null_row
    slope_out[...] = embed_sig * (1.0 + pre_embed * (1.0 - embed_sig))

    row_group = jnp.floor(
        (lax.broadcasted_iota(jnp.int32, (channels, channels), 0).astype(F32) + 0.5) * (1.0 / group_width)
    )
    col_group = jnp.floor(
        (lax.broadcasted_iota(jnp.int32, (channels, channels), 1).astype(F32) + 0.5) * (1.0 / group_width)
    )
    same[...] = jnp.where(row_group == col_group, 1.0, 0.0).astype(BF16)

    wait_all(stat_copies, stat_send, stat_recv, stat_ssem, stat_rsem)
    all_sums = stat_recv[:, :, :channels]
    total_sum = jnp.sum(all_sums, axis=0)
    grid_cells = cells * n
    group_count = grid_cells * group_width
    chan_mean = total_sum * (1.0 / grid_cells)
    off = all_sums * (1.0 / cells) - chan_mean[None]
    chan_m2 = jnp.sum(stat_recv[:, :, channels:] + cells * (off * off), axis=0)
    hid_mean = chan_mean + proj
    (mean_total,) = group_sums([hid_mean], same)
    group_mean = mean_total * (1.0 / group_width)
    shift = hid_mean - group_mean
    (var_total,) = group_sums([chan_m2 + grid_cells * (shift * shift)], same)
    group_var = var_total * (1.0 / group_count)
    inv_std = 1.0 / jnp.sqrt(group_var + 1e-05)
    normed_sum = shift * inv_std * grid_cells

    col_index = lax.broadcasted_iota(jnp.int32, (columns, channels), 0)

    def spread_columns(block, place, buffer, flip):
        left = jnp.where(col_index == 0, 0.0, pltpu.roll(block, 1, 0))
        right = jnp.where(col_index == columns - 1, 0.0, pltpu.roll(block, columns - 1, 0))
        if flip:
            left, right = right, left
        for b, part in enumerate((left, block, right)):
            buffer[pl.ds(place, columns), b * channels : (b + 1) * channels] = part.astype(BF16)

    def normalised(block):
        return ((block.astype(F32) + proj) - group_mean) * inv_std

    def own_row(r, carry):
        place = pl.multiple_of(r * columns, columns)
        value = normalised(hidden[pl.ds(place, columns), :])
        sig = jax.nn.sigmoid(value)
        normed[pl.ds(place, columns), :] = value
        spread_columns(value * sig, pl.multiple_of(place + columns, columns), field, False)
        return carry

    lax.fori_loop(0, cells // columns, own_row, 0)

    wait_halo(raw_halo)

    def outside(place, buffer):
        buffer[pl.ds(place, columns), :] = jnp.zeros((columns, 3 * channels), BF16)

    for ref, place, inside in ((hid_low, 0, has_low), (hid_high, cells + columns, has_high)):

        @pl.when(inside)
        def _():
            value = normalised(ref[...])
            spread_columns(value * jax.nn.sigmoid(value), place, field, False)

        pl.when(jnp.logical_not(inside))(functools.partial(outside, place, field))

    for copy in loads[4:]:
        copy.wait()
    col_tall = lax.rem(lax.broadcasted_iota(jnp.int32, (cells, 256), 0), columns)
    depth = 3 * channels
    loss_part = jnp.zeros((1, 1), F32)
    tiles = tiles_of(channels, 256)
    head = tiles[-1][0]
    cot_halo = [
        halo_copies(
            edge_send.at[0, :, lanes], edge_send.at[1, :, lanes], edge_low.at[:, lanes], edge_high.at[:, lanes],
            cot_ssem, cot_rsem, 2 * piece,
        )
        for piece, lanes in enumerate((pl.ds(0, head), pl.ds(head, channels - head)))
    ]
    for start, width in tiles:
        if start == head:
            start_halo(cot_halo[0])
        acc = None
        for a in range(3):
            part = jnp.dot(
                field[a * columns : a * columns + cells, :],
                conv[a * depth : (a + 1) * depth, start : start + width],
                preferred_element_type=F32,
            )
            acc = part if acc is None else acc + part
        out = (skip[:, start : start + width].astype(F32) + acc).astype(BF16)
        pred[:, start : start + width] = out
        error = out.astype(F32) - target[:, start : start + width].astype(F32)
        loss_part = loss_part + jnp.sum(error * error, keepdims=True)
        rounded = error.astype(BF16)
        wide = rounded.astype(F32)
        near = col_tall[:, :width]
        after = jnp.where(near == columns - 1, 0.0, pltpu.roll(wide, cells - 1, 0)).astype(BF16)
        before = jnp.where(near == 0, 0.0, pltpu.roll(wide, 1, 0)).astype(BF16)
        for b, part in enumerate((after, rounded, before)):
            cot[columns : columns + cells, b * channels + start : b * channels + start + width] = part
        edge_send[0, :, start : start + width] = rounded[:columns]
        edge_send[1, :, start : start + width] = rounded[cells - columns :]

    start_halo(cot_halo[1])

    def back_tap(a, start, width, acc):
        for b in range(3):
            base = (a * 3 + b) * channels + start
            part = lax.dot_general(
                cot[(2 - a) * columns : (2 - a) * columns + cells, b * channels : (b + 1) * channels],
                conv[base : base + width, :],
                (((1,), (1,)), ((), ())),
                preferred_element_type=F32,
            )
            acc = part if acc is None else acc + part
        return acc

    for start, width in tiles:
        partial[:, start : start + width] = back_tap(1, start, width, None)

    for pair in cot_halo:
        wait_halo(pair)
    for ref, place, inside in ((edge_low, 0, has_low), (edge_high, cells + columns, has_high)):

        @pl.when(inside)
        def _():
            spread_columns(ref[...].astype(F32), place, cot, True)

        pl.when(jnp.logical_not(inside))(functools.partial(outside, place, cot))

    head_copies = []
    for start, width in tiles:
        if start == head:
            head_send[:, 2 * head :] = jnp.broadcast_to(loss_part, (1, 128))
            head_copies = send_all(head_send, head_recv, head_ssem, head_rsem)
            head_recv[me] = head_send[...]
        acc = back_tap(2, start, width, back_tap(0, start, width, None)) + partial[:, start : start + width]
        value = normed[:, start : start + width]
        sig = jax.nn.sigmoid(value)
        grad = acc * (sig * (1.0 + value * (1.0 - sig)))
        cross = grad * value
        dest, place, span = (tail_send, 0, width) if start == head else (head_send, start, head)
        dest[:, place : place + width] = jnp.sum(grad, axis=0, keepdims=True)
        dest[:, span + place : span + place + width] = jnp.sum(cross, axis=0, keepdims=True)

    tail_copies = send_all(tail_send, tail_recv, tail_ssem, tail_rsem)
    tail_recv[me] = tail_send[...]
    wait_all(head_copies, head_send, head_recv, head_ssem, head_rsem)
    early = jnp.sum(head_recv[...], axis=0)
    wait_all(tail_copies, tail_send, tail_recv, tail_ssem, tail_rsem)
    late = jnp.sum(tail_recv[...], axis=0)
    rest = channels - head
    grad_chan = jnp.concatenate([early[:, :head], late[:, :rest]], axis=1)
    cross_chan = jnp.concatenate([early[:, head : 2 * head], late[:, rest:]], axis=1)
    grad_groups, cross_groups = group_sums([grad_chan, cross_chan], same)
    mean_grad = grad_groups * (1.0 / group_count)
    mean_cross = cross_groups * (1.0 / group_count)
    grad_proj = (grad_chan - mean_grad * grid_cells - mean_cross * normed_sum) * inv_std
    proj_out[...] = grad_proj
    loss_out[...] = early[:, 2 * head :] * (1.0 / (grid_cells * channels))
    for copy in stat_copies + head_copies + tail_copies:
        copy.wait_send()


def finish(pred_ref, embed_ref, proj_ref, loss_in, null_ref, slope_ref, pred_hbm, loss_ref, new_ref, sem):
    copy = pltpu.make_async_copy(pred_ref, pred_hbm, sem)
    copy.start()
    back = lax.dot_general(
        pieces([proj_ref[...]]), embed_ref[...], (((1,), (1,)), ((), ())), preferred_element_type=F32
    )
    grad_null = joined(back, 1)[0] * slope_ref[...]
    width = grad_null.shape[1]
    scale = 0.5 / jnp.sqrt(jnp.sum(grad_null * grad_null, keepdims=True) * (1.0 / width) + 1e-06)
    new_ref[...] = (null_ref[...] - grad_null * scale).reshape(width)
    loss_ref[...] = jnp.sum(loss_in[:, :1], axis=1)
    copy.wait()


def body(n, skip_input, conv_hidden, noise_target, timestep, tile_id, tile_table, null_embed, embed_weight, conv_weight):
    rows_local, columns, channels = skip_input.shape
    cells = rows_local * columns
    width = null_embed.shape[0]
    any_spec = pl.BlockSpec(memory_space=pl.ANY)
    vmem = pl.BlockSpec(memory_space=pltpu.VMEM)
    smem = pl.BlockSpec(memory_space=pltpu.SMEM)
    dma = pltpu.SemaphoreType.DMA
    padded = cells + 2 * columns
    head = tiles_of(channels, 256)[-1][0]
    held = pl.pallas_call(
        functools.partial(kernel, n, columns),
        out_shape=(
            pltpu.VMEM((cells, channels), BF16),
            pltpu.VMEM((width, channels), BF16),
            pltpu.VMEM((1, channels), F32),
            pltpu.VMEM((1, 128), F32),
            pltpu.VMEM((1, width), F32),
            pltpu.VMEM((1, width), F32),
        ),
        in_specs=[smem] * 2 + [any_spec] * 7,
        out_specs=(vmem,) * 6,
        scratch_shapes=[
            pltpu.VMEM((cells, channels), BF16),
            pltpu.VMEM((cells, channels), BF16),
            pltpu.VMEM((cells, channels), BF16),
            pltpu.VMEM((9 * channels, channels), BF16),
            pltpu.VMEM(tile_table.shape, F32),
            pltpu.VMEM((width,), F32),
            pltpu.VMEM((padded, 3 * channels), BF16),
            pltpu.VMEM((padded, 3 * channels), BF16),
            pltpu.VMEM((cells, channels), F32),
            pltpu.VMEM((2, columns, channels), BF16),
            pltpu.VMEM((columns, channels), BF16),
            pltpu.VMEM((columns, channels), BF16),
            pltpu.VMEM((columns, channels), BF16),
            pltpu.VMEM((columns, channels), BF16),
            pltpu.VMEM((channels, channels), BF16),
            pltpu.VMEM((cells, channels), F32),
            pltpu.VMEM((1, 2 * channels), F32),
            pltpu.VMEM((n, 1, 2 * channels), F32),
            pltpu.VMEM((1, 2 * head + 128), F32),
            pltpu.VMEM((n, 1, 2 * head + 128), F32),
            pltpu.VMEM((1, 2 * (channels - head)), F32),
            pltpu.VMEM((n, 1, 2 * (channels - head)), F32),
            dma((7,)), *[dma((n,))] * 6, dma((2,)), dma((2,)), dma((4,)), dma((4,)),
        ],
        compiler_params=pltpu.CompilerParams(
            collective_id=0, has_side_effects=True, vmem_limit_bytes=40 * 1024 * 1024
        ),
        name="resblock_step",
    )(timestep, tile_id, *[pltpu.with_memory_space_constraint(part, pltpu.HBM) for part in (
        conv_hidden.reshape(cells, channels), skip_input.reshape(cells, channels),
        noise_target.reshape(cells, channels), conv_weight.reshape(9 * channels, channels),
        embed_weight, tile_table, null_embed,
    )])
    held = [pltpu.with_memory_space_constraint(part, pltpu.VMEM) for part in held]
    pred, loss, new_null = pl.pallas_call(
        finish,
        out_shape=(
            jax.ShapeDtypeStruct((cells, channels), BF16),
            jax.ShapeDtypeStruct((1,), F32),
            jax.ShapeDtypeStruct((width,), F32),
        ),
        in_specs=[vmem] * 6,
        out_specs=(any_spec, vmem, vmem),
        scratch_shapes=[dma],
        compiler_params=pltpu.CompilerParams(vmem_limit_bytes=16 * 1024 * 1024),
        name="resblock_finish",
    )(*held)
    return pred.reshape(rows_local, columns, channels), loss, new_null


def solution(mesh):
    rows = P(("groups", "rows"), None, None)
    in_specs = (rows, rows, rows, P("groups"), P("groups"), P(), P("groups"), P(), P())
    out_specs = (rows, P("groups"), P("groups"))
    return jax.shard_map(
        functools.partial(body, mesh.shape["rows"]),
        mesh=mesh, in_specs=in_specs, out_specs=out_specs, check_vma=False,
    )
```

```python
import functools
import math

import jax
import jax.numpy as jnp
from jax import lax
from jax.experimental import pallas as pl
from jax.experimental.pallas import tpu as pltpu
from jax.sharding import PartitionSpec as P

GROUPS = 32
MESH = pl.DeviceIdType.MESH
F32 = jnp.float32
BF16 = jnp.bfloat16


def pieces(rows):
    out = []
    for row in rows:
        for _ in range(3):
            part = row.astype(BF16).astype(F32)
            out.append(part)
            row = row - part
    height = 16
    index = lax.broadcasted_iota(jnp.int32, (height, rows[0].shape[1]), 0)
    block = jnp.zeros((height, rows[0].shape[1]), F32)
    for place, part in enumerate(out):
        block = jnp.where(index == place, part, block)
    return block.astype(BF16)


def joined(product, count):
    return [
        product[3 * k : 3 * k + 1] + product[3 * k + 1 : 3 * k + 2] + product[3 * k + 2 : 3 * k + 3]
        for k in range(count)
    ]


def group_sums(rows, same_ref):
    product = jnp.dot(pieces(rows), same_ref[...], preferred_element_type=F32)
    return joined(product, len(rows))


def tiles_of(extent, width):
    return [(start, min(width, extent - start)) for start in range(0, extent, width)]


def kernel(
    n, columns,
    time_ref, tile_ref, hidden_hbm, skip_hbm, target_hbm, conv_hbm, embed_hbm, table_hbm, null_hbm,
    pred, embed, proj_out, loss_out, null_out, slope_out,
    hidden, skip, target, conv, conv_back, table_ref, null_ref, field, cot, normed, edge_send, edge_low, edge_high,
    hid_low, hid_high, same, partial, stat_send, stat_recv, head_send, head_recv, tail_send, tail_recv,
    load_sem, stat_ssem, stat_rsem, head_ssem, head_rsem, tail_ssem, tail_rsem, halo_ssem, halo_rsem, cot_ssem, cot_rsem,
):
    me = lax.axis_index("rows")
    cells, channels = hidden.shape
    group_width = channels // GROUPS
    half = null_ref.shape[0] // 2
    has_low, has_high = me > 0, me < n - 1

    barrier = pltpu.get_barrier_semaphore()
    for k in range(1, n):
        pl.semaphore_signal(barrier, inc=1, device_id={"rows": lax.rem(me + k, n)}, device_id_type=MESH)

    loads = []
    for place, (src, dst) in enumerate(
        (
            (hidden_hbm, hidden), (null_hbm, null_ref),
            (table_hbm, table_ref), (embed_hbm, embed), (conv_hbm, conv), (skip_hbm, skip), (target_hbm, target),
        )
    ):
        copy = pltpu.make_async_copy(src, dst, load_sem.at[place])
        copy.start()
        loads.append(copy)
    turned_loads = []
    for a in range(3):
        for b in range(3):
            copy = pltpu.make_async_copy(
                conv_hbm.at[pl.ds((3 * a + b) * channels, channels), :],
                conv_back.at[pl.ds(a * channels, channels), pl.ds(b * channels, channels)],
                load_sem.at[7 + 3 * a + b],
            )
            copy.start()
            turned_loads.append(copy)
    loads[0].wait()

    raw = hidden[...].astype(F32)
    chan_sum = jnp.sum(raw, axis=0, keepdims=True)
    spread = raw - chan_sum * (1.0 / cells)
    chan_sq = jnp.sum(spread * spread, axis=0, keepdims=True)
    stat_send[:, :channels] = chan_sum
    stat_send[:, channels:] = chan_sq

    pl.semaphore_wait(barrier, n - 1)

    def send_all(src, recv, ssem, rsem):
        copies = []
        for k in range(1, n):
            copy = pltpu.make_async_remote_copy(
                src_ref=src, dst_ref=recv.at[me], send_sem=ssem.at[k], recv_sem=rsem.at[me],
                device_id={"rows": lax.rem(me + k, n)}, device_id_type=MESH,
            )
            copy.start()
            copies.append(copy)
        return copies

    def wait_all(copies, src, recv, ssem, rsem):
        for k in range(1, n):
            sender = lax.rem(me + k, n)
            pltpu.make_async_remote_copy(
                src_ref=src, dst_ref=recv.at[sender], send_sem=ssem.at[k], recv_sem=rsem.at[sender],
                device_id={"rows": sender}, device_id_type=MESH,
            ).wait_recv()

    stat_copies = send_all(stat_send, stat_recv, stat_ssem, stat_rsem)
    stat_recv[me] = stat_send[...]

    def halo_copies(low_src, high_src, low_dst, high_dst, ssem, rsem, place=0):
        down = pltpu.make_async_remote_copy(
            src_ref=low_src, dst_ref=high_dst, send_sem=ssem.at[place], recv_sem=rsem.at[place],
            device_id={"rows": lax.rem(me + n - 1, n)}, device_id_type=MESH,
        )
        up = pltpu.make_async_remote_copy(
            src_ref=high_src, dst_ref=low_dst, send_sem=ssem.at[place + 1], recv_sem=rsem.at[place + 1],
            device_id={"rows": lax.rem(me + 1, n)}, device_id_type=MESH,
        )
        return down, up

    def start_halo(pair):
        pl.when(has_low)(pair[0].start)
        pl.when(has_high)(pair[1].start)

    def wait_halo(pair):
        pl.when(has_low)(pair[0].wait_send)
        pl.when(has_high)(pair[1].wait_send)
        pl.when(has_high)(pair[0].wait_recv)
        pl.when(has_low)(pair[1].wait_recv)

    raw_halo = halo_copies(
        hidden.at[pl.ds(0, columns)], hidden.at[pl.ds(cells - columns, columns)],
        hid_low, hid_high, halo_ssem, halo_rsem,
    )
    start_halo(raw_halo)

    index = lax.broadcasted_iota(jnp.int32, (1, half), 1).astype(F32)
    freqs = jnp.exp(-math.log(10000.0) * index / half)
    for copy in loads[1:3]:
        copy.wait()
    null_row = null_ref[...].reshape(1, 2 * half)
    phase = time_ref[0].astype(F32) * freqs
    tile_row = lax.broadcasted_iota(jnp.int32, table_ref.shape, 0)
    picked = jnp.sum(jnp.where(tile_row == tile_ref[0], table_ref[...], 0.0), axis=0, keepdims=True)
    pre_embed = null_row + jnp.concatenate([jnp.cos(phase), jnp.sin(phase)], axis=1) + picked
    embed_sig = jax.nn.sigmoid(pre_embed)
    act_embed = jnp.broadcast_to((pre_embed * embed_sig), (16, 2 * half)).astype(BF16)
    loads[3].wait()
    proj = jnp.dot(act_embed, embed[...], preferred_element_type=F32)[0:1]
    null_out[...] = null_row
    slope_out[...] = embed_sig * (1.0 + pre_embed * (1.0 - embed_sig))

    row_group = jnp.floor(
        (lax.broadcasted_iota(jnp.int32, (channels, channels), 0).astype(F32) + 0.5) * (1.0 / group_width)
    )
    col_group = jnp.floor(
        (lax.broadcasted_iota(jnp.int32, (channels, channels), 1).astype(F32) + 0.5) * (1.0 / group_width)
    )
    same[...] = jnp.where(row_group == col_group, 1.0, 0.0).astype(BF16)

    wait_all(stat_copies, stat_send, stat_recv, stat_ssem, stat_rsem)
    all_sums = stat_recv[:, :, :channels]
    total_sum = jnp.sum(all_sums, axis=0)
    grid_cells = cells * n
    group_count = grid_cells * group_width
    chan_mean = total_sum * (1.0 / grid_cells)
    off = all_sums * (1.0 / cells) - chan_mean[None]
    chan_m2 = jnp.sum(stat_recv[:, :, channels:] + cells * (off * off), axis=0)
    hid_mean = chan_mean + proj
    (mean_total,) = group_sums([hid_mean], same)
    group_mean = mean_total * (1.0 / group_width)
    shift = hid_mean - group_mean
    (var_total,) = group_sums([chan_m2 + grid_cells * (shift * shift)], same)
    group_var = var_total * (1.0 / group_count)
    inv_std = 1.0 / jnp.sqrt(group_var + 1e-05)
    normed_sum = shift * inv_std * grid_cells

    col_index = lax.broadcasted_iota(jnp.int32, (columns, channels), 0)

    def spread_columns(block, place, buffer, flip):
        left = jnp.where(col_index == 0, 0.0, pltpu.roll(block, 1, 0))
        right = jnp.where(col_index == columns - 1, 0.0, pltpu.roll(block, columns - 1, 0))
        if flip:
            left, right = right, left
        for b, part in enumerate((left, block, right)):
            buffer[pl.ds(place, columns), b * channels : (b + 1) * channels] = part.astype(BF16)

    def normalised(block):
        return ((block.astype(F32) + proj) - group_mean) * inv_std

    def own_row(r, carry):
        place = pl.multiple_of(r * columns, columns)
        value = normalised(hidden[pl.ds(place, columns), :])
        sig = jax.nn.sigmoid(value)
        normed[pl.ds(place, columns), :] = value
        spread_columns(value * sig, pl.multiple_of(place + columns, columns), field, False)
        return carry

    lax.fori_loop(0, cells // columns, own_row, 0)

    wait_halo(raw_halo)

    def outside(place, buffer):
        buffer[pl.ds(place, columns), :] = jnp.zeros((columns, 3 * channels), BF16)

    for ref, place, inside in ((hid_low, 0, has_low), (hid_high, cells + columns, has_high)):

        @pl.when(inside)
        def _():
            value = normalised(ref[...])
            spread_columns(value * jax.nn.sigmoid(value), place, field, False)

        pl.when(jnp.logical_not(inside))(functools.partial(outside, place, field))

    for copy in loads[4:]:
        copy.wait()
    col_tall = lax.rem(lax.broadcasted_iota(jnp.int32, (cells, 256), 0), columns)
    depth = 3 * channels
    loss_part = jnp.zeros((1, 1), F32)
    tiles = tiles_of(channels, 256)
    head = tiles[-1][0]
    cot_halo = [
        halo_copies(
            edge_send.at[0, :, lanes], edge_send.at[1, :, lanes], edge_low.at[:, lanes], edge_high.at[:, lanes],
            cot_ssem, cot_rsem, 2 * piece,
        )
        for piece, lanes in enumerate((pl.ds(0, head), pl.ds(head, channels - head)))
    ]
    for start, width in tiles:
        if start == head:
            start_halo(cot_halo[0])
        acc = None
        for a in range(3):
            part = jnp.dot(
                field[a * columns : a * columns + cells, :],
                conv[a * depth : (a + 1) * depth, start : start + width],
                preferred_element_type=F32,
            )
            acc = part if acc is None else acc + part
        out = (skip[:, start : start + width].astype(F32) + acc).astype(BF16)
        pred[:, start : start + width] = out
        error = out.astype(F32) - target[:, start : start + width].astype(F32)
        loss_part = loss_part + jnp.sum(error * error, keepdims=True)
        rounded = error.astype(BF16)
        wide = rounded.astype(F32)
        near = col_tall[:, :width]
        after = jnp.where(near == columns - 1, 0.0, pltpu.roll(wide, cells - 1, 0)).astype(BF16)
        before = jnp.where(near == 0, 0.0, pltpu.roll(wide, 1, 0)).astype(BF16)
        for b, part in enumerate((after, rounded, before)):
            cot[columns : columns + cells, b * channels + start : b * channels + start + width] = part
        edge_send[0, :, start : start + width] = rounded[:columns]
        edge_send[1, :, start : start + width] = rounded[cells - columns :]

    start_halo(cot_halo[1])

    def back_tap(a, start, width, acc):
        part = lax.dot_general(
            cot[(2 - a) * columns : (2 - a) * columns + cells, :],
            conv_back[a * channels + start : a * channels + start + width, :],
            (((1,), (1,)), ((), ())),
            preferred_element_type=F32,
        )
        return part if acc is None else acc + part

    for copy in turned_loads:
        copy.wait()
    for start, width in tiles:
        partial[:, start : start + width] = back_tap(1, start, width, None)

    for pair in cot_halo:
        wait_halo(pair)
    for ref, place, inside in ((edge_low, 0, has_low), (edge_high, cells + columns, has_high)):

        @pl.when(inside)
        def _():
            spread_columns(ref[...].astype(F32), place, cot, True)

        pl.when(jnp.logical_not(inside))(functools.partial(outside, place, cot))

    head_copies = []
    for start, width in tiles:
        if start == head:
            head_send[:, 2 * head :] = jnp.broadcast_to(loss_part, (1, 128))
            head_copies = send_all(head_send, head_recv, head_ssem, head_rsem)
            head_recv[me] = head_send[...]
        acc = back_tap(2, start, width, back_tap(0, start, width, None)) + partial[:, start : start + width]
        value = normed[:, start : start + width]
        sig = jax.nn.sigmoid(value)
        grad = acc * (sig * (1.0 + value * (1.0 - sig)))
        cross = grad * value
        dest, place, span = (tail_send, 0, width) if start == head else (head_send, start, head)
        dest[:, place : place + width] = jnp.sum(grad, axis=0, keepdims=True)
        dest[:, span + place : span + place + width] = jnp.sum(cross, axis=0, keepdims=True)

    tail_copies = send_all(tail_send, tail_recv, tail_ssem, tail_rsem)
    tail_recv[me] = tail_send[...]
    wait_all(head_copies, head_send, head_recv, head_ssem, head_rsem)
    early = jnp.sum(head_recv[...], axis=0)
    wait_all(tail_copies, tail_send, tail_recv, tail_ssem, tail_rsem)
    late = jnp.sum(tail_recv[...], axis=0)
    rest = channels - head
    grad_chan = jnp.concatenate([early[:, :head], late[:, :rest]], axis=1)
    cross_chan = jnp.concatenate([early[:, head : 2 * head], late[:, rest:]], axis=1)
    grad_groups, cross_groups = group_sums([grad_chan, cross_chan], same)
    mean_grad = grad_groups * (1.0 / group_count)
    mean_cross = cross_groups * (1.0 / group_count)
    grad_proj = (grad_chan - mean_grad * grid_cells - mean_cross * normed_sum) * inv_std
    proj_out[...] = grad_proj
    loss_out[...] = early[:, 2 * head :] * (1.0 / (grid_cells * channels))
    for copy in stat_copies + head_copies + tail_copies:
        copy.wait_send()


def finish(pred_ref, embed_ref, proj_ref, loss_in, null_ref, slope_ref, pred_hbm, loss_ref, new_ref, sem):
    copy = pltpu.make_async_copy(pred_ref, pred_hbm, sem)
    copy.start()
    back = lax.dot_general(
        pieces([proj_ref[...]]), embed_ref[...], (((1,), (1,)), ((), ())), preferred_element_type=F32
    )
    grad_null = joined(back, 1)[0] * slope_ref[...]
    width = grad_null.shape[1]
    scale = 0.5 / jnp.sqrt(jnp.sum(grad_null * grad_null, keepdims=True) * (1.0 / width) + 1e-06)
    new_ref[...] = (null_ref[...] - grad_null * scale).reshape(width)
    loss_ref[...] = jnp.sum(loss_in[:, :1], axis=1)
    copy.wait()


def body(n, skip_input, conv_hidden, noise_target, timestep, tile_id, tile_table, null_embed, embed_weight, conv_weight):
    rows_local, columns, channels = skip_input.shape
    cells = rows_local * columns
    width = null_embed.shape[0]
    any_spec = pl.BlockSpec(memory_space=pl.ANY)
    vmem = pl.BlockSpec(memory_space=pltpu.VMEM)
    smem = pl.BlockSpec(memory_space=pltpu.SMEM)
    dma = pltpu.SemaphoreType.DMA
    padded = cells + 2 * columns
    head = tiles_of(channels, 256)[-1][0]
    held = pl.pallas_call(
        functools.partial(kernel, n, columns),
        out_shape=(
            pltpu.VMEM((cells, channels), BF16),
            pltpu.VMEM((width, channels), BF16),
            pltpu.VMEM((1, channels), F32),
            pltpu.VMEM((1, 128), F32),
            pltpu.VMEM((1, width), F32),
            pltpu.VMEM((1, width), F32),
        ),
        in_specs=[smem] * 2 + [any_spec] * 7,
        out_specs=(vmem,) * 6,
        scratch_shapes=[
            pltpu.VMEM((cells, channels), BF16),
            pltpu.VMEM((cells, channels), BF16),
            pltpu.VMEM((cells, channels), BF16),
            pltpu.VMEM((9 * channels, channels), BF16),
            pltpu.VMEM((3 * channels, 3 * channels), BF16),
            pltpu.VMEM(tile_table.shape, F32),
            pltpu.VMEM((width,), F32),
            pltpu.VMEM((padded, 3 * channels), BF16),
            pltpu.VMEM((padded, 3 * channels), BF16),
            pltpu.VMEM((cells, channels), F32),
            pltpu.VMEM((2, columns, channels), BF16),
            pltpu.VMEM((columns, channels), BF16),
            pltpu.VMEM((columns, channels), BF16),
            pltpu.VMEM((columns, channels), BF16),
            pltpu.VMEM((columns, channels), BF16),
            pltpu.VMEM((channels, channels), BF16),
            pltpu.VMEM((cells, channels), F32),
            pltpu.VMEM((1, 2 * channels), F32),
            pltpu.VMEM((n, 1, 2 * channels), F32),
            pltpu.VMEM((1, 2 * head + 128), F32),
            pltpu.VMEM((n, 1, 2 * head + 128), F32),
            pltpu.VMEM((1, 2 * (channels - head)), F32),
            pltpu.VMEM((n, 1, 2 * (channels - head)), F32),
            dma((16,)), *[dma((n,))] * 6, dma((2,)), dma((2,)), dma((4,)), dma((4,)),
        ],
        compiler_params=pltpu.CompilerParams(
            collective_id=0, has_side_effects=True, vmem_limit_bytes=40 * 1024 * 1024
        ),
        name="resblock_step",
    )(timestep, tile_id, *[pltpu.with_memory_space_constraint(part, pltpu.HBM) for part in (
        conv_hidden.reshape(cells, channels), skip_input.reshape(cells, channels),
        noise_target.reshape(cells, channels), conv_weight.reshape(9 * channels, channels),
        embed_weight, tile_table, null_embed,
    )])
    held = [pltpu.with_memory_space_constraint(part, pltpu.VMEM) for part in held]
    pred, loss, new_null = pl.pallas_call(
        finish,
        out_shape=(
            jax.ShapeDtypeStruct((cells, channels), BF16),
            jax.ShapeDtypeStruct((1,), F32),
            jax.ShapeDtypeStruct((width,), F32),
        ),
        in_specs=[vmem] * 6,
        out_specs=(any_spec, vmem, vmem),
        scratch_shapes=[dma],
        compiler_params=pltpu.CompilerParams(vmem_limit_bytes=16 * 1024 * 1024),
        name="resblock_finish",
    )(*held)
    return pred.reshape(rows_local, columns, channels), loss, new_null


def solution(mesh):
    rows = P(("groups", "rows"), None, None)
    in_specs = (rows, rows, rows, P("groups"), P("groups"), P(), P("groups"), P(), P())
    out_specs = (rows, P("groups"), P("groups"))
    return jax.shard_map(
        functools.partial(body, mesh.shape["rows"]),
        mesh=mesh, in_specs=in_specs, out_specs=out_specs, check_vma=False,
    )
```
